32 devices in a mesh: dp: 4 (over y, core), tensor: 8 (over z, x).
Axes of the slice: x: 2, y: 2, z: 4, core: 2. Of those that a mesh axis runs over, the one named last changes fastest.
Arguments:
- out_grad: bfloat16 [2048, 4096], P(('dp', 'tensor')), may hold values from -6 to 6
- gate_pre: bfloat16 [2048, 16384], P('dp', 'tensor'), may hold values from -6 to 6
- up_pre: bfloat16 [2048, 16384], P('dp', 'tensor'), may hold values from -6 to 6
- gate_codes: int32 [1024, 16384], P(None, 'tensor'), may hold values from 0 to 65280
- up_codes: int32 [1024, 16384], P(None, 'tensor'), may hold values from 0 to 65280
- down_codes: int32 [16384, 1024], P('tensor'), may hold values from 0 to 65280
- gate_scale: float32 [32, 16384], P(None, 'tensor'), may hold values from 0.00171875 to 0.006875
- up_scale: float32 [32, 16384], P(None, 'tensor'), may hold values from 0.00171875 to 0.006875
- down_scale: float32 [128, 4096], P('tensor'), may hold values from 0.000859375 to 0.0034375
- weak_weight: bfloat16 [256, 4096], P('tensor'), may hold values from -0.125 to 0.125
- weak_index: int32 [256], P('tensor'), may hold values from -1 to 2047, as said below
Outputs:
- in_grad: bfloat16 [2048, 4096], P(('dp', 'tensor'))
- weak_grad: float32 [256, 4096], P('tensor', 'dp')
The draws below stay inside these ranges and needn't reach their ends.
Inputs may be any that keep to these rules, and one draw needn't show every extreme that they name: `weak_index`: slot s belongs to tensor rank s // 32. A rank's live slots come first and hold distinct hidden units of that rank, counted from 0; its other slots hold -1. Counts of live slots differ from rank to rank, and some rank has all 32 slots live.
All inputs are finite; a program needn't handle non-finite values.
Results may differ from the reference program's by a relative error of at most 0.017.
Values may be sent and summed in bfloat16 or wider, within the bound.
A program may use at most 256 MiB of HBM per device.

```python
import math
import jax
import jax.numpy as jnp

D = 4096
FF = 16384
GROUP = 128
WMAX = 32
TOKENS = 2048
FF_RANK = 2048
WEAK_SLOTS = 256


def pick_units(unit_key):
    return jax.random.permutation(unit_key, FF_RANK - 1)[:WMAX]


def draw_weak_index(key, part):
    rank_count = WEAK_SLOTS // WMAX
    key_count, key_full, key_units = jax.random.split(key, 3)
    counts = jax.random.randint(key_count, (rank_count,), 1, WMAX // 2 + 1)
    full_rank = jax.random.randint(key_full, (), 0, rank_count)
    is_full = jnp.arange(rank_count) == full_rank
    counts = jnp.where(is_full, WMAX, counts)
    unit_order = jax.vmap(pick_units)(jax.random.split(key_units, rank_count))
    slot_number = jnp.arange(WMAX)[None, :]
    first_slot = (slot_number == 0) & is_full[:, None]
    unit_order = jnp.where(first_slot, FF_RANK - 1, unit_order)
    chosen = jnp.where(slot_number < counts[:, None], unit_order, -1)
    return chosen.reshape(-1).astype(jnp.int32)


def place_ends(result, key, smallest, top_value):
    longest = result.shape.index(max(result.shape))
    spots = []
    for shift in (0, 1):
        where = [jax.random.randint(jax.random.fold_in(key, axis), (), 0, length) for axis, length in enumerate(result.shape)]
        where[longest] = (where[longest] + shift) % result.shape[longest]
        spots.append(tuple(where))
    return result.at[spots[0]].set(smallest).at[spots[1]].set(top_value)


def steps_of(rng, extent, cuts, smallest, largest):
    loudness = 1.0
    for dim, blocks in cuts:
        steps = jax.random.uniform(jax.random.fold_in(jax.random.fold_in(rng, 6), dim), (blocks,), jnp.float32, smallest / len(cuts), largest / len(cuts))
        loudness = loudness * jnp.repeat(jnp.exp(steps), extent[dim] // blocks).reshape((-1,) + (1,) * (len(extent) - 1 - dim))
    return loudness


def bell_draw(own_key, dims, width, bound, pieces=(), kind=jnp.bfloat16):
    level = steps_of(own_key, dims, pieces, -0.22, 0.18) if pieces else 1.0
    values = jax.random.normal(own_key, dims, jnp.float32) * width * level
    return jnp.minimum(jnp.maximum(values, -bound), bound).astype(kind)


def setup_inputs(seed: int = 0) -> dict:
    splits = jax.random.split(jax.random.key(seed), 12)
    out_grad = bell_draw(splits[0], (TOKENS, D), 1.0, 6.0, ((0, 32),))
    gate_pre = bell_draw(splits[1], (TOKENS, FF), 1.0, 6.0, ((0, 4), (1, 8)))
    up_pre = bell_draw(splits[2], (TOKENS, FF), 1.0, 6.0, ((0, 4), (1, 8)))
    gate_codes = place_ends(jax.random.randint(splits[3], (D // 4, FF), 0, 65281), jax.random.fold_in(splits[3], 1), 0, 65280).astype(jnp.int32)
    up_codes = place_ends(jax.random.randint(splits[4], (D // 4, FF), 0, 65281), jax.random.fold_in(splits[4], 1), 0, 65280).astype(jnp.int32)
    down_codes = place_ends(jax.random.randint(splits[5], (FF, D // 4), 0, 65281), jax.random.fold_in(splits[5], 1), 0, 65280).astype(jnp.int32)
    gate_scale = jnp.clip(jnp.exp(math.log(0.006875) - 1.3862944 * jax.random.uniform(splits[6], (D // GROUP, FF), jnp.float32) ** steps_of(splits[6], (D // GROUP, FF), ((1, 8),), -0.2, 0.2)), 0.00171875, 0.006875)
    up_scale = jnp.clip(jnp.exp(math.log(0.006875) - 1.3862944 * jax.random.uniform(splits[7], (D // GROUP, FF), jnp.float32) ** steps_of(splits[7], (D // GROUP, FF), ((1, 8),), -0.2, 0.2)), 0.00171875, 0.006875)
    down_scale = jnp.clip(jnp.exp(math.log(0.0034375) - 1.3862944 * jax.random.uniform(splits[8], (FF // GROUP, D), jnp.float32) ** steps_of(splits[8], (FF // GROUP, D), ((0, 8),), -0.2, 0.2)), 0.000859375, 0.0034375)
    weak_weight = bell_draw(splits[9], (WEAK_SLOTS, D), (FF // 9) ** -0.5, 0.125, ((0, 8),))
    weak_index = draw_weak_index(jax.random.fold_in(splits[11], 71), 0)
    return {"out_grad": out_grad, "gate_pre": gate_pre, "up_pre": up_pre, "gate_codes": gate_codes, "up_codes": up_codes, "down_codes": down_codes, "gate_scale": gate_scale, "up_scale": up_scale, "down_scale": down_scale, "weak_weight": weak_weight, "weak_index": weak_index}


def unpack_levels(packed, unpack_axis):
    nibble_slabs = [(packed // (16 ** nibble)) % 16 for nibble in range(4)]
    return jnp.concatenate(nibble_slabs, axis=unpack_axis).astype(jnp.float32)


def dequant(packed, group_scale, unpack_axis):
    levels = unpack_levels(packed, unpack_axis)
    height, breadth = levels.shape
    groups = group_scale.shape[0]
    grouped = (levels - 7.5).reshape(groups, height // groups, breadth) * group_scale[:, None, :]
    return grouped.reshape(height, breadth)


def reference(out_grad, gate_pre, up_pre, gate_codes, up_codes, down_codes, gate_scale, up_scale, down_scale, weak_weight, weak_index):
    w_gate = dequant(gate_codes, gate_scale, 0).astype(jnp.bfloat16)
    w_up = dequant(up_codes, up_scale, 0).astype(jnp.bfloat16)
    down_plain = dequant(down_codes, down_scale, 1)
    slot_rank = jnp.arange(WEAK_SLOTS, dtype=jnp.int32) // WMAX
    weak_unit = jnp.where(weak_index >= 0, slot_rank * FF_RANK + weak_index, -1).astype(jnp.int32)
    select_mask = jnp.arange(FF, dtype=jnp.int32)[:, None] == weak_unit[None, :]
    select = select_mask.astype(jnp.bfloat16)
    weak_rows = jnp.dot(select, weak_weight, preferred_element_type=jnp.float32)
    is_weak = jnp.any(select_mask, axis=1)
    w_down = jnp.where(is_weak[:, None], weak_rows, down_plain).astype(jnp.bfloat16)
    hidden_grad = jnp.dot(out_grad, w_down.T, preferred_element_type=jnp.float32)
    gate_value = gate_pre.astype(jnp.float32)
    up_value = up_pre.astype(jnp.float32)
    sigmoid_gate = jax.nn.sigmoid(gate_value)
    activated = gate_value * sigmoid_gate
    up_grad = (hidden_grad * activated).astype(jnp.bfloat16)
    gate_grad = (hidden_grad * up_value * sigmoid_gate * (1.0 + gate_value * (1.0 - sigmoid_gate))).astype(jnp.bfloat16)
    in_grad = jnp.dot(gate_grad, w_gate.T, preferred_element_type=jnp.float32) + jnp.dot(up_grad, w_up.T, preferred_element_type=jnp.float32)
    hidden = (activated * up_value).astype(jnp.bfloat16)
    hidden_weak = jnp.dot(hidden, select, preferred_element_type=jnp.float32).astype(jnp.bfloat16)
    weak_grad = jnp.dot(hidden_weak.T, out_grad, preferred_element_type=jnp.float32) * (TOKENS ** -0.5)
    return in_grad.astype(jnp.bfloat16), weak_grad
```

```python
import functools

import jax
import jax.numpy as jnp
from jax import lax
from jax.experimental import pallas as pl
from jax.experimental.pallas import tpu as pltpu
from jax.sharding import PartitionSpec as P

BF = jnp.bfloat16
F32 = jnp.float32
NT = (((1,), (1,)), ((), ()))


def params(mib=40):
    return pltpu.CompilerParams(
        dimension_semantics=("arbitrary",), vmem_limit_bytes=mib * 1024 * 1024
    )


def cost(flops, nbytes, trans=0):
    return pl.CostEstimate(flops=flops, bytes_accessed=nbytes, transcendentals=trans)


def deq_cols_kernel(per_slab, codes_ref, scale_ref, out_ref):
    block = pl.program_id(0)
    rows = codes_ref.shape[0]

    @pl.loop(0, rows // 16)
    def _(piece):
        at = pl.ds(pl.multiple_of(piece * 16, 16), 16)
        codes = codes_ref[at, :]
        for nibble in range(4):
            level = ((codes >> (4 * nibble)) & 15).astype(F32) - 7.5
            scale = scale_ref[pl.ds(nibble * per_slab + block, 1), :]
            out_ref[nibble, at, :] = (level * scale).astype(BF)


def deq_cols(codes, scale):
    packed_rows, width = codes.shape
    groups = scale.shape[0]
    group = 4 * packed_rows // groups
    out = pl.pallas_call(
        functools.partial(deq_cols_kernel, groups // 4),
        grid=(packed_rows // group,),
        in_specs=[
            pl.BlockSpec((group, width), lambda r: (r, 0)),
            pl.BlockSpec((groups, width), lambda r: (0, 0)),
        ],
        out_specs=pl.BlockSpec((4, group, width), lambda r: (0, r, 0)),
        out_shape=jax.ShapeDtypeStruct((4, packed_rows, width), BF),
        compiler_params=params(58),
        cost_estimate=cost(packed_rows * width * 24, packed_rows * width * 12),
        name="deq_cols",
    )(codes, scale)
    return out.reshape(4 * packed_rows, width)


def deq_rows_kernel(codes_ref, scale_ref, weak_ref, index_ref, out_ref):
    block = pl.program_id(0)
    rows, packed = codes_ref.shape
    slots = weak_ref.shape[0]
    index = index_ref[...]
    first = block * rows
    unit = lax.broadcasted_iota(jnp.int32, (rows, slots), 0) + first
    onehot = (unit == index).astype(F32).astype(BF)
    for nibble in range(4):
        cols = slice(nibble * packed, (nibble + 1) * packed)
        out_ref[:, cols] = jnp.dot(
            onehot, weak_ref[:, cols], preferred_element_type=F32
        ).astype(BF)

    @pl.loop(0, rows // 16)
    def _(piece):
        at = pl.ds(pl.multiple_of(piece * 16, 16), 16)
        codes = codes_ref[at, :]
        here = lax.broadcasted_iota(jnp.int32, (16, slots), 0) + (first + piece * 16)
        hit = jnp.max((here == index).astype(F32), axis=1, keepdims=True) > 0.5
        for nibble in range(4):
            cols = slice(nibble * packed, (nibble + 1) * packed)
            level = ((codes >> (4 * nibble)) & 15).astype(F32) - 7.5
            plain = level * scale_ref[pl.ds(block, 1), cols]
            out_ref[at, cols] = jnp.where(hit, out_ref[at, cols].astype(F32), plain).astype(BF)


def deq_rows(codes, scale, weak, index_row):
    units, packed = codes.shape
    groups, width = scale.shape
    group = units // groups
    slots = weak.shape[0]
    return pl.pallas_call(
        deq_rows_kernel,
        grid=(groups,),
        in_specs=[
            pl.BlockSpec((group, packed), lambda r: (r, 0)),
            pl.BlockSpec((groups, width), lambda r: (0, 0)),
            pl.BlockSpec((slots, width), lambda r: (0, 0)),
            pl.BlockSpec((1, slots), lambda r: (0, 0)),
        ],
        out_specs=pl.BlockSpec((group, width), lambda r: (r, 0)),
        out_shape=jax.ShapeDtypeStruct((units, width), BF),
        compiler_params=params(58),
        cost_estimate=cost(units * width * 8, units * packed * 12),
        name="deq_rows",
    )(codes, scale, weak, index_row)


def hidden_kernel(places, count, rows, *refs):
    pieces = refs[1 : 1 + len(places)]
    rest = refs[1 + len(places) :]
    w_ref, col_ref = rest[0], rest[1]
    gates = rest[2 : 2 + count]
    ups = rest[2 + count : 2 + 2 * count]
    gg_ref, ug_ref, weak_ref, tokens, picked = rest[2 + 2 * count :]
    step = pl.program_id(0)
    width = w_ref.shape[0]
    slots = col_ref.shape[0]

    @pl.when(step == 0)
    def _():
        for (row, col), piece in zip(places, pieces):
            tokens[row * rows : (row + 1) * rows, col : col + piece.shape[1]] = piece[...]
        picked[...] = jnp.zeros_like(picked)

    grad = lax.dot_general(tokens[...], w_ref[...], NT, preferred_element_type=F32)
    unit = lax.broadcasted_iota(jnp.int32, (slots, width), 1) + step * width
    onehot = (unit == col_ref[...]).astype(F32).astype(BF)
    hiddens = []
    for k in range(count):
        mine = slice(k * rows, (k + 1) * rows)
        gate = gates[k][...].astype(F32)
        up = ups[k][...].astype(F32)
        sig = 1.0 / (1.0 + jnp.exp(-gate))
        act = gate * sig
        part = grad[mine]
        ug_ref[mine, :] = (part * act).astype(BF)
        gg_ref[mine, :] = (part * up * sig * (1.0 + gate * (1.0 - sig))).astype(BF)
        hiddens.append((act * up).astype(BF))
    hidden = jnp.concatenate(hiddens, axis=0)
    picked[...] += lax.dot_general(onehot, hidden, NT, preferred_element_type=F32)

    @pl.when(step == pl.num_programs(0) - 1)
    def _():
        weak_ref[...] = jnp.dot(
            picked[...].astype(BF), tokens[...], preferred_element_type=F32
        )


def hidden_stage(ids, places, pieces, w_down, index_col, gate_pre, up_pre):
    count = ids.shape[0]
    rows = pieces[0].shape[0]
    units, model = w_down.shape
    slots = index_col.shape[0]
    width = min(256, units)
    total = count * rows
    pre_specs = [
        pl.BlockSpec((rows, width), functools.partial(lambda k, f, who: (who[k], f), k))
        for k in range(count)
    ]
    return pl.pallas_call(
        functools.partial(hidden_kernel, places, count, rows),
        grid_spec=pltpu.PrefetchScalarGridSpec(
            num_scalar_prefetch=1,
            grid=(units // width,),
            in_specs=[pl.BlockSpec(p.shape, lambda f, who: (0, 0)) for p in pieces]
            + [
                pl.BlockSpec((width, model), lambda f, who: (f, 0)),
                pl.BlockSpec((slots, 1), lambda f, who: (0, 0)),
            ]
            + pre_specs
            + pre_specs,
            out_specs=[
                pl.BlockSpec((total, width), lambda f, who: (0, f)),
                pl.BlockSpec((total, width), lambda f, who: (0, f)),
                pl.BlockSpec((slots, model), lambda f, who: (0, 0)),
            ],
            scratch_shapes=[pltpu.VMEM((total, model), BF), pltpu.VMEM((slots, total), F32)],
        ),
        out_shape=[
            jax.ShapeDtypeStruct((total, units), BF),
            jax.ShapeDtypeStruct((total, units), BF),
            jax.ShapeDtypeStruct((slots, model), F32),
        ],
        compiler_params=params(),
        cost_estimate=cost(
            2 * total * units * model, 2 * (units * model + 4 * total * units), total * units * 2
        ),
        name="hidden_stage",
    )(ids, *pieces, w_down, index_col, *([gate_pre] * count), *([up_pre] * count))


def input_kernel(gg_ref, ug_ref, wg_ref, wu_ref, out_ref):
    total = lax.dot_general(gg_ref[...], wg_ref[...], NT, preferred_element_type=F32)
    total += lax.dot_general(ug_ref[...], wu_ref[...], NT, preferred_element_type=F32)
    out_ref[...] = total.astype(BF)


def input_stage(gg, ug, w_gate, w_up, half):
    total, units = gg.shape
    model = w_gate.shape[0]
    width = min(256, model // 2)
    steps = model // 2 // width
    w_spec = pl.BlockSpec((width, units), lambda i: (half * steps + i, 0))
    g_spec = pl.BlockSpec((total, units), lambda i: (0, 0))
    return pl.pallas_call(
        input_kernel,
        grid=(steps,),
        in_specs=[g_spec, g_spec, w_spec, w_spec],
        out_specs=pl.BlockSpec((total, width), lambda i: (0, i)),
        out_shape=jax.ShapeDtypeStruct((total, model // 2), BF),
        compiler_params=params(),
        cost_estimate=cost(2 * total * units * model, 2 * units * model),
        name="input_stage",
    )(gg, ug, w_gate, w_up)


def per_device(
    out_grad,
    gate_pre,
    up_pre,
    gate_codes,
    up_codes,
    down_codes,
    gate_scale,
    up_scale,
    down_scale,
    weak_weight,
    weak_index,
):
    n = lax.axis_size("tensor")
    groups = lax.axis_size("dp")
    half = n // 2
    rows, model = out_grad.shape
    middle = model // 2

    order = [2 * p if p < half else 2 * (n - 1 - p) + 1 for p in range(n)]
    to_right = [(order[p], order[(p + 1) % n]) for p in range(n)]
    to_left = [(order[(p + 1) % n], order[p]) for p in range(n)]
    me = lax.axis_index("tensor")
    position = jnp.where(me % 2 == 0, me // 2, n - 1 - me // 2)

    def who(offset):
        p = (position + offset + n) % n
        return jnp.where(p < half, 2 * p, 2 * (n - 1 - p) + 1)

    right = lambda x: lax.ppermute(x, "tensor", to_right)
    left = lambda x: lax.ppermute(x, "tensor", to_left)

    index = weak_index.astype(jnp.int32)
    weights = [
        lambda: deq_rows(down_codes, down_scale, weak_weight, index[None, :]),
        lambda: deq_cols(gate_codes, gate_scale),
        lambda: deq_cols(up_codes, up_scale),
    ]
    ready = []

    blocks = {0: [(0, out_grad)]}
    from_left, from_right = out_grad, out_grad
    for hop in range(1, half):
        from_left, from_right = right(from_left), left(from_right)
        if weights:
            ready.append(weights.pop(0)())
            from_left, from_right, ready[-1] = lax.optimization_barrier(
                (from_left, from_right, ready[-1])
            )
        blocks[-hop] = [(0, from_left)]
        blocks[hop] = [(0, from_right)]
    while weights:
        ready.append(weights.pop(0)())
    w_down, w_gate, w_up = ready
    blocks[half] = [(0, right(from_left[:, :middle])), (middle, left(from_right[:, middle:]))]

    sequence = [o for hop in range(1, half) for o in (-hop, hop)] + [half, 0]
    chunks = [sequence[:half], sequence[half:]]

    sums = {}
    weak = None
    for chunk in chunks:
        ids = jnp.stack([who(o) for o in chunk]).astype(jnp.int32)
        places, pieces = [], []
        for k, o in enumerate(chunk):
            for col, piece in blocks[o]:
                places.append((k, col))
                pieces.append(piece)
        gg, ug, part = hidden_stage(ids, places, pieces, w_down, index[:, None], gate_pre, up_pre)
        weak = part if weak is None else weak + part
        for side in (0, 1):
            out = input_stage(gg, ug, w_gate, w_up, side)
            for k, o in enumerate(chunk):
                sums[o, side] = out[k * rows : (k + 1) * rows]

    def wrap(offset):
        offset %= n
        return offset if offset <= half else offset - n

    ends = []
    for side, send, sign in ((0, right, -1), (1, left, 1)):
        moving = sums[wrap(sign), side]
        for step in range(2, n + 1):
            arrived = send(moving)
            own = sums[wrap(sign * step), side]
            moving = (arrived.astype(F32) + own.astype(F32)).astype(BF)
        ends.append(moving)
    in_grad = jnp.concatenate(ends, axis=1)

    slots = weak.shape[0]
    mine = lax.axis_index("dp")
    width = model // groups
    cut = lambda g: lax.dynamic_slice(weak, (0, g * width), (slots, width))
    total = cut(mine)
    for shift in range(1, groups):
        sent = cut((mine + shift) % groups).astype(BF)
        total += lax.ppermute(
            sent, "dp", [(g, (g + shift) % groups) for g in range(groups)]
        ).astype(F32)
    factor = (gate_pre.shape[0] * groups) ** (-0.5)
    return in_grad, total * factor


def solution(mesh):
    in_specs = (
        P(("dp", "tensor"), None),
        P("dp", "tensor"),
        P("dp", "tensor"),
        P(None, "tensor"),
        P(None, "tensor"),
        P("tensor", None),
        P(None, "tensor"),
        P(None, "tensor"),
        P("tensor", None),
        P("tensor", None),
        P("tensor"),
    )
    out_specs = (P(("dp", "tensor"), None), P("tensor", "dp"))
    return jax.shard_map(
        per_device, mesh=mesh, in_specs=in_specs, out_specs=out_specs, check_vma=False
    )
```

```python
import functools

import jax
import jax.numpy as jnp
from jax import lax
from jax.experimental import pallas as pl
from jax.experimental.pallas import tpu as pltpu
from jax.sharding import PartitionSpec as P

BF = jnp.bfloat16
F32 = jnp.float32
NT = (((1,), (1,)), ((), ()))


def params(mib=40):
    return pltpu.CompilerParams(
        dimension_semantics=("arbitrary",), vmem_limit_bytes=mib * 1024 * 1024
    )


def cost(flops, nbytes, trans=0):
    return pl.CostEstimate(flops=flops, bytes_accessed=nbytes, transcendentals=trans)


def deq_cols_kernel(per_slab, codes_ref, scale_ref, out_ref):
    block = pl.program_id(0)
    rows, width = codes_ref.shape
    piece = min(512, width)

    for nibble in range(4):
        unit = 16.0**nibble
        for col in range(0, width, piece):
            cols = slice(col, col + piece)
            scale = scale_ref[pl.ds(nibble * per_slab + block, 1), cols] * (1.0 / unit)
            scale = jnp.broadcast_to(scale, (16, piece))
            for row in range(0, rows, 16):
                at = slice(row, row + 16)
                level = (codes_ref[at, cols] & (15 << (4 * nibble))).astype(F32) - 7.5 * unit
                out_ref[nibble, at, cols] = (level * scale).astype(BF)


def deq_cols(codes, scale):
    packed_rows, width = codes.shape
    groups = scale.shape[0]
    group = 4 * packed_rows // groups
    out = pl.pallas_call(
        functools.partial(deq_cols_kernel, groups // 4),
        grid=(packed_rows // group,),
        in_specs=[
            pl.BlockSpec((group, width), lambda r: (r, 0)),
            pl.BlockSpec((groups, width), lambda r: (0, 0)),
        ],
        out_specs=pl.BlockSpec((4, group, width), lambda r: (0, r, 0)),
        out_shape=jax.ShapeDtypeStruct((4, packed_rows, width), BF),
        compiler_params=params(58),
        cost_estimate=cost(packed_rows * width * 24, packed_rows * width * 12),
        name="deq_cols",
    )(codes, scale)
    return out.reshape(4 * packed_rows, width)


def deq_rows_kernel(index_ref, codes_ref, scale_ref, weak_ref, out_ref):
    block = pl.program_id(0)
    rows, packed = codes_ref.shape
    slots, model = weak_ref.shape
    piece = min(512, packed)
    for nibble in range(4):
        unit = 16.0**nibble
        for col in range(0, packed, piece):
            cols = slice(col, col + piece)
            outs = slice(nibble * packed + col, nibble * packed + col + piece)
            scale = jnp.broadcast_to(scale_ref[pl.ds(block, 1), outs] * (1.0 / unit), (16, piece))
            for row in range(0, rows, 16):
                at = slice(row, row + 16)
                level = (codes_ref[at, cols] & (15 << (4 * nibble))).astype(F32) - 7.5 * unit
                out_ref[at, outs] = (level * scale).astype(BF)

    @pl.loop(0, slots)
    def _(slot):
        unit = index_ref[slot] - block * rows

        @pl.when((unit >= 0) & (unit < rows))
        def _():
            at = pl.ds(pl.multiple_of(unit // 16 * 16, 16), 16)
            hit = lax.broadcasted_iota(jnp.int32, (16, piece), 0) == unit % 16
            for col in range(0, model, piece):
                cols = slice(col, col + piece)
                row = jnp.broadcast_to(weak_ref[pl.ds(slot, 1), cols], (16, piece))
                out_ref[at, cols] = jnp.where(hit, row, out_ref[at, cols].astype(F32)).astype(BF)


def deq_rows(codes, scale, weak, index):
    units, packed = codes.shape
    groups, width = scale.shape
    group = units // groups
    slots = weak.shape[0]
    return pl.pallas_call(
        deq_rows_kernel,
        grid_spec=pltpu.PrefetchScalarGridSpec(
            num_scalar_prefetch=1,
            grid=(groups,),
            in_specs=[
                pl.BlockSpec((group, packed), lambda r, index: (r, 0)),
                pl.BlockSpec((groups, width), lambda r, index: (0, 0)),
                pl.BlockSpec((slots, width), lambda r, index: (0, 0)),
            ],
            out_specs=pl.BlockSpec((group, width), lambda r, index: (r, 0)),
        ),
        out_shape=jax.ShapeDtypeStruct((units, width), BF),
        compiler_params=params(58),
        cost_estimate=cost(units * width * 8, units * packed * 12),
        name="deq_rows",
    )(index, codes, scale, weak.astype(F32))


def hidden_kernel(places, count, rows, *refs):
    pieces = refs[1 : 1 + len(places)]
    rest = refs[1 + len(places) :]
    w_ref, col_ref = rest[0], rest[1]
    gates = rest[2 : 2 + count]
    ups = rest[2 + count : 2 + 2 * count]
    gg_ref, ug_ref, weak_ref, tokens, picked = rest[2 + 2 * count :]
    step = pl.program_id(0)
    width = w_ref.shape[0]
    slots = col_ref.shape[0]

    @pl.when(step == 0)
    def _():
        for (row, col), piece in zip(places, pieces):
            tokens[row * rows : (row + 1) * rows, col : col + piece.shape[1]] = piece[...]
        picked[...] = jnp.zeros_like(picked)

    grad = lax.dot_general(tokens[...], w_ref[...], NT, preferred_element_type=F32)
    unit = lax.broadcasted_iota(jnp.int32, (slots, width), 1) + step * width
    onehot = (unit == col_ref[...]).astype(F32).astype(BF)
    hiddens = []
    for k in range(count):
        mine = slice(k * rows, (k + 1) * rows)
        gate = gates[k][...].astype(F32)
        up = ups[k][...].astype(F32)
        sig = 1.0 / (1.0 + jnp.exp(-gate))
        act = gate * sig
        part = grad[mine]
        ug_ref[mine, :] = (part * act).astype(BF)
        gg_ref[mine, :] = (part * up * sig * (1.0 + gate * (1.0 - sig))).astype(BF)
        hiddens.append((act * up).astype(BF))
    hidden = jnp.concatenate(hiddens, axis=0)
    picked[...] += lax.dot_general(onehot, hidden, NT, preferred_element_type=F32)

    @pl.when(step == pl.num_programs(0) - 1)
    def _():
        weak_ref[...] = jnp.dot(
            picked[...].astype(BF), tokens[...], preferred_element_type=F32
        )


def hidden_stage(ids, places, pieces, w_down, index_col, gate_pre, up_pre):
    count = ids.shape[0]
    rows = pieces[0].shape[0]
    units, model = w_down.shape
    slots = index_col.shape[0]
    width = min(256, units)
    total = count * rows
    pre_specs = [
        pl.BlockSpec((rows, width), functools.partial(lambda k, f, who: (who[k], f), k))
        for k in range(count)
    ]
    return pl.pallas_call(
        functools.partial(hidden_kernel, places, count, rows),
        grid_spec=pltpu.PrefetchScalarGridSpec(
            num_scalar_prefetch=1,
            grid=(units // width,),
            in_specs=[pl.BlockSpec(p.shape, lambda f, who: (0, 0)) for p in pieces]
            + [
                pl.BlockSpec((width, model), lambda f, who: (f, 0)),
                pl.BlockSpec((slots, 1), lambda f, who: (0, 0)),
            ]
            + pre_specs
            + pre_specs,
            out_specs=[
                pl.BlockSpec((total, width), lambda f, who: (0, f)),
                pl.BlockSpec((total, width), lambda f, who: (0, f)),
                pl.BlockSpec((slots, model), lambda f, who: (0, 0)),
            ],
            scratch_shapes=[pltpu.VMEM((total, model), BF), pltpu.VMEM((slots, total), F32)],
        ),
        out_shape=[
            jax.ShapeDtypeStruct((total, units), BF),
            jax.ShapeDtypeStruct((total, units), BF),
            jax.ShapeDtypeStruct((slots, model), F32),
        ],
        compiler_params=params(),
        cost_estimate=cost(
            2 * total * units * model, 2 * (units * model + 4 * total * units), total * units * 2
        ),
        name="hidden_stage",
    )(ids, *pieces, w_down, index_col, *([gate_pre] * count), *([up_pre] * count))


def ring_device(p, n):
    back = p // (n // 2)
    return (1 - back) * (2 * p) + back * (2 * (n - 1 - p) + 1)


def ring_position(index, n):
    odd = index % 2
    return (1 - odd) * (index // 2) + odd * (n - 1 - index // 2)


def scatter_kernel(
    n, blocks, gg_ref, ug_ref, wg_ref, wu_ref, out_ref, part, slots, send_sem, recv_sem
):
    step = pl.program_id(0)
    rows, model = out_ref.shape
    width = model // blocks
    position = ring_position(lax.axis_index("tensor"), n)
    right = ring_device((position + 1) % n, n)
    left = ring_device((position + n - 1) % n, n)

    @pl.when(step == 0)
    def _():
        barrier = pltpu.get_barrier_semaphore()
        for other in (left, right):
            pl.semaphore_signal(
                barrier, inc=1, device_id={"tensor": other}, device_id_type=pl.DeviceIdType.MESH
            )
        pl.semaphore_wait(barrier, 2)

    def copy(block, hop, source):
        return pltpu.make_async_remote_copy(
            src_ref=source,
            dst_ref=slots.at[block, hop],
            send_sem=send_sem.at[block, hop],
            recv_sem=recv_sem.at[block, hop],
            device_id={"tensor": right if block % 2 == 0 else left},
            device_id_type=pl.DeviceIdType.MESH,
        )

    for block in range(blocks):
        hop = step - 1 - block
        place = (n - 1 - hop) if block % 2 == 0 else (hop + 1) % n

        @pl.when(hop == 0)
        def _():
            copy(block, 0, part.at[block, n - 1 if block % 2 == 0 else 1]).start()

        @pl.when((hop > 0) & (hop < n))
        def _():
            before = hop - 1
            copy(block, before, slots.at[block, before]).wait()
            own = part[block, place].astype(F32)
            total = (slots[block, before].astype(F32) + own).astype(BF)

            @pl.when(hop < n - 1)
            def _():
                slots[block, before] = total
                copy(block, hop, slots.at[block, before]).start()

            @pl.when(hop == n - 1)
            def _():
                out_ref[:, block * width : (block + 1) * width] = total

    @pl.when(step < blocks)
    def _():
        total = lax.dot_general(gg_ref[...], wg_ref[...], NT, preferred_element_type=F32)
        total += lax.dot_general(ug_ref[...], wu_ref[...], NT, preferred_element_type=F32)
        part[step] = total.astype(BF).reshape(n, rows, width)


def input_scatter(gg, ug, w_gate, w_up, n):
    tokens, units = gg.shape
    model = w_gate.shape[0]
    rows = tokens // n
    blocks = 8
    width = model // blocks
    g_spec = pl.BlockSpec((tokens, units), lambda i: (0, 0), pipeline_mode=pl.Buffered(1))
    w_spec = pl.BlockSpec((width, units), lambda i: (jnp.minimum(i, blocks - 1), 0))
    return pl.pallas_call(
        functools.partial(scatter_kernel, n, blocks),
        grid=(blocks + n,),
        in_specs=[g_spec, g_spec, w_spec, w_spec],
        out_specs=pl.BlockSpec((rows, model), lambda i: (0, 0)),
        out_shape=jax.ShapeDtypeStruct((rows, model), BF),
        scratch_shapes=[
            pltpu.VMEM((blocks, n, rows, width), BF),
            pltpu.VMEM((blocks, n - 1, rows, width), BF),
            pltpu.SemaphoreType.DMA((blocks, n - 1)),
            pltpu.SemaphoreType.DMA((blocks, n - 1)),
        ],
        compiler_params=pltpu.CompilerParams(
            dimension_semantics=("arbitrary",),
            vmem_limit_bytes=50 * 1024 * 1024,
            collective_id=0,
            has_side_effects=True,
        ),
        cost_estimate=cost(4 * tokens * units * model, 4 * units * model),
        name="input_scatter",
    )(gg, ug, w_gate, w_up)


def per_device(
    out_grad,
    gate_pre,
    up_pre,
    gate_codes,
    up_codes,
    down_codes,
    gate_scale,
    up_scale,
    down_scale,
    weak_weight,
    weak_index,
):
    n = lax.axis_size("tensor")
    groups = lax.axis_size("dp")
    half = n // 2
    rows, model = out_grad.shape
    middle = model // 2

    order = [2 * p if p < half else 2 * (n - 1 - p) + 1 for p in range(n)]
    to_right = [(order[p], order[(p + 1) % n]) for p in range(n)]
    to_left = [(order[(p + 1) % n], order[p]) for p in range(n)]
    me = lax.axis_index("tensor")
    position = ring_position(me, n)

    right = lambda x: lax.ppermute(x, "tensor", to_right)
    left = lambda x: lax.ppermute(x, "tensor", to_left)

    index = weak_index.astype(jnp.int32)
    weights = [
        lambda: deq_rows(down_codes, down_scale, weak_weight, index),
        lambda: deq_cols(gate_codes, gate_scale),
        lambda: deq_cols(up_codes, up_scale),
    ]
    ready = []

    blocks = {0: [(0, out_grad)]}
    from_left, from_right = out_grad, out_grad
    for hop in range(1, half):
        from_left, from_right = right(from_left), left(from_right)
        if weights:
            ready.append(weights.pop(0)())
            from_left, from_right, ready[-1] = lax.optimization_barrier(
                (from_left, from_right, ready[-1])
            )
        blocks[-hop] = [(0, from_left)]
        blocks[hop] = [(0, from_right)]
    while weights:
        ready.append(weights.pop(0)())
    w_down, w_gate, w_up = ready
    blocks[half] = [(0, right(from_left[:, :middle])), (middle, left(from_right[:, middle:]))]

    places, pieces = [], []
    for offset in range(n):
        for col, piece in blocks[offset if offset <= half else offset - n]:
            places.append((offset, col))
            pieces.append(piece)
    ids = ring_device((position + jnp.arange(n, dtype=jnp.int32)) % n, n)
    gg, ug, weak = hidden_stage(ids, places, pieces, w_down, index[:, None], gate_pre, up_pre)
    in_grad = input_scatter(gg, ug, w_gate, w_up, n)

    slots = weak.shape[0]
    mine = lax.axis_index("dp")
    width = model // groups
    cut = lambda g: lax.dynamic_slice(weak, (0, g * width), (slots, width))
    total = cut(mine)
    for shift in range(1, groups):
        sent = cut((mine + shift) % groups).astype(BF)
        total += lax.ppermute(
            sent, "dp", [(g, (g + shift) % groups) for g in range(groups)]
        ).astype(F32)
    factor = (gate_pre.shape[0] * groups) ** (-0.5)
    return in_grad, total * factor


def solution(mesh):
    in_specs = (
        P(("dp", "tensor"), None),
        P("dp", "tensor"),
        P("dp", "tensor"),
        P(None, "tensor"),
        P(None, "tensor"),
        P("tensor", None),
        P(None, "tensor"),
        P(None, "tensor"),
        P("tensor", None),
        P("tensor", None),
        P("tensor"),
    )
    out_specs = (P(("dp", "tensor"), None), P("tensor", "dp"))
    return jax.shard_map(
        per_device, mesh=mesh, in_specs=in_specs, out_specs=out_specs, check_vma=False
    )
```

```python
import functools

import jax
import jax.numpy as jnp
from jax import lax
from jax.experimental import pallas as pl
from jax.experimental.pallas import tpu as pltpu
from jax.sharding import PartitionSpec as P

BF = jnp.bfloat16
F32 = jnp.float32
NT = (((1,), (1,)), ((), ()))


def params(mib=60):
    return pltpu.CompilerParams(
        dimension_semantics=("arbitrary",), vmem_limit_bytes=mib * 1024 * 1024
    )


def cost(flops, nbytes, trans=0):
    return pl.CostEstimate(flops=flops, bytes_accessed=nbytes, transcendentals=trans)


def deq_rows_kernel(first, index_ref, codes_ref, scale_ref, weak_ref, *refs):
    out_ref = refs[-1]
    block = pl.program_id(0) + first
    rows, packed = codes_ref.shape
    slots, model = weak_ref.shape
    piece = min(512, packed)
    for nibble in range(4):
        unit = 16.0**nibble
        for col in range(0, packed, piece):
            cols = slice(col, col + piece)
            outs = slice(nibble * packed + col, nibble * packed + col + piece)
            scale = jnp.broadcast_to(scale_ref[pl.ds(block, 1), outs] * (1.0 / unit), (16, piece))
            for row in range(0, rows, 16):
                at = slice(row, row + 16)
                level = (codes_ref[at, cols] & (15 << (4 * nibble))).astype(F32) - 7.5 * unit
                out_ref[at, outs] = (level * scale).astype(BF)

    @pl.loop(0, slots)
    def _(slot):
        unit = index_ref[slot] - block * rows

        @pl.when((unit >= 0) & (unit < rows))
        def _():
            at = pl.ds(pl.multiple_of(unit // 16 * 16, 16), 16)
            hit = lax.broadcasted_iota(jnp.int32, (16, piece), 0) == unit % 16
            for col in range(0, model, piece):
                cols = slice(col, col + piece)
                row = jnp.broadcast_to(weak_ref[pl.ds(slot, 1), cols], (16, piece))
                out_ref[at, cols] = jnp.where(hit, row, out_ref[at, cols].astype(F32)).astype(BF)


def deq_rows(codes, scale, weak, index, first, count, before=None):
    units, packed = codes.shape
    groups, width = scale.shape
    group = units // groups
    slots = weak.shape[0]
    more = [] if before is None else [before]
    return pl.pallas_call(
        functools.partial(deq_rows_kernel, first),
        grid_spec=pltpu.PrefetchScalarGridSpec(
            num_scalar_prefetch=1,
            grid=(count,),
            in_specs=[
                pl.BlockSpec((group, packed), lambda r, index: (r + first, 0)),
                pl.BlockSpec((groups, width), lambda r, index: (0, 0)),
                pl.BlockSpec((slots, width), lambda r, index: (0, 0)),
            ]
            + [pl.BlockSpec(memory_space=pl.ANY)] * len(more),
            out_specs=pl.BlockSpec((group, width), lambda r, index: (r + first, 0)),
        ),
        out_shape=jax.ShapeDtypeStruct((units, width), BF),
        input_output_aliases={4: 0} if more else {},
        compiler_params=params(),
        cost_estimate=cost(count * group * width * 8, count * group * packed * 12),
        name="deq_rows",
    )(index, codes, scale, weak, *more)


def hidden_kernel(places, count, rows, *refs):
    pieces = refs[1 : 1 + len(places)]
    rest = refs[1 + len(places) :]
    w_ref, col_ref = rest[0], rest[1]
    gates = rest[2 : 2 + count]
    ups = rest[2 + count : 2 + 2 * count]
    gg_ref, ug_ref, weak_ref, tokens, picked = rest[-5:]
    step = pl.program_id(0)
    width = w_ref.shape[0]
    slots = col_ref.shape[0]

    @pl.when(step == 0)
    def _():
        for (row, col), piece in zip(places, pieces):
            tokens[row * rows : (row + 1) * rows, col : col + piece.shape[1]] = piece[...]
        picked[...] = jnp.zeros_like(picked)

    grad = lax.dot_general(tokens[...], w_ref[...], NT, preferred_element_type=F32)
    unit = lax.broadcasted_iota(jnp.int32, (slots, width), 1) + step * width
    onehot = (unit == col_ref[...]).astype(F32).astype(BF)
    hiddens = []
    for k in range(count):
        mine = slice(k * rows, (k + 1) * rows)
        gate = gates[k][...].astype(F32)
        up = ups[k][...].astype(F32)
        sig = 1.0 / (1.0 + jnp.exp(-gate))
        act = gate * sig
        part = grad[mine]
        ug_ref[mine, :] = (part * act).astype(BF)
        gg_ref[mine, :] = (part * up * sig * (1.0 + gate * (1.0 - sig))).astype(BF)
        hiddens.append((act * up).astype(BF))
    hidden = jnp.concatenate(hiddens, axis=0)
    picked[...] += lax.dot_general(onehot, hidden, NT, preferred_element_type=F32)

    @pl.when(step == pl.num_programs(0) - 1)
    def _():
        weak_ref[...] = jnp.dot(
            picked[...].astype(BF), tokens[...], preferred_element_type=F32
        )


def hidden_stage(chunk, chunks, ids, places, pieces, w_down, index_col, gate_pre, up_pre, before=()):
    count = ids.shape[0]
    rows = pieces[0].shape[0]
    units, model = w_down.shape
    slots = index_col.shape[0]
    width = min(256, units)
    total = count * rows
    pre_specs = [
        pl.BlockSpec((rows, width), functools.partial(lambda k, f, who: (who[k], f), k))
        for k in range(count)
    ]
    return pl.pallas_call(
        functools.partial(hidden_kernel, places, count, rows),
        grid_spec=pltpu.PrefetchScalarGridSpec(
            num_scalar_prefetch=1,
            grid=(units // width,),
            in_specs=[pl.BlockSpec(p.shape, lambda f, who: (0, 0)) for p in pieces]
            + [
                pl.BlockSpec((width, model), lambda f, who: (f, 0)),
                pl.BlockSpec((slots, 1), lambda f, who: (0, 0)),
            ]
            + pre_specs
            + pre_specs
            + [pl.BlockSpec(memory_space=pl.ANY)] * len(before),
            out_specs=[
                pl.BlockSpec((total, width), lambda f, who: (chunk, f)),
                pl.BlockSpec((total, width), lambda f, who: (chunk, f)),
                pl.BlockSpec((slots, model), lambda f, who: (0, 0)),
            ],
            scratch_shapes=[pltpu.VMEM((total, model), BF), pltpu.VMEM((slots, total), F32)],
        ),
        out_shape=[
            jax.ShapeDtypeStruct((chunks * total, units), BF),
            jax.ShapeDtypeStruct((chunks * total, units), BF),
            jax.ShapeDtypeStruct((slots, model), F32),
        ],
        input_output_aliases={3 + len(pieces) + 2 * count + k: k for k in range(len(before))},
        compiler_params=params(),
        cost_estimate=cost(
            2 * total * units * model, 2 * (units * model + 4 * total * units), total * units * 2
        ),
        name="hidden_stage",
    )(ids, *pieces, w_down, index_col, *([gate_pre] * count), *([up_pre] * count), *before)


def ring_device(p, n):
    back = p // (n // 2)
    return (1 - back) * (2 * p) + back * (2 * (n - 1 - p) + 1)


def ring_position(index, n):
    odd = index % 2
    return (1 - odd) * (index // 2) + odd * (n - 1 - index // 2)


def scatter_kernel(
    n,
    blocks,
    sequence,
    gg_ref,
    ug_ref,
    gc_ref,
    uc_ref,
    gs_ref,
    us_ref,
    out_ref,
    part,
    slots,
    weights,
    send_sem,
    recv_sem,
):
    step = pl.program_id(0)
    rows, model = out_ref.shape
    width, units = gc_ref.shape
    groups = gs_ref.shape[0]
    group = model // groups
    position = ring_position(lax.axis_index("tensor"), n)
    right = ring_device((position + 1) % n, n)
    left = ring_device((position + n - 1) % n, n)

    @pl.when(step == 0)
    def _():
        barrier = pltpu.get_barrier_semaphore()
        for other in (left, right):
            pl.semaphore_signal(
                barrier, inc=1, device_id={"tensor": other}, device_id_type=pl.DeviceIdType.MESH
            )
        pl.semaphore_wait(barrier, 2)

    def copy(block, hop, source):
        return pltpu.make_async_remote_copy(
            src_ref=source,
            dst_ref=slots.at[block, hop],
            send_sem=send_sem.at[block, hop],
            recv_sem=recv_sem.at[block, hop],
            device_id={"tensor": right if block % 2 == 0 else left},
            device_id_type=pl.DeviceIdType.MESH,
        )

    for block in range(blocks):
        hop = step - 1 - block
        place = (n - 1 - hop) if block % 2 == 0 else (hop + 1) % n

        @pl.when(hop == 0)
        def _():
            copy(block, 0, part.at[block, n - 1 if block % 2 == 0 else 1]).start()

        @pl.when((hop > 0) & (hop < n))
        def _():
            before = hop - 1
            copy(block, before, slots.at[block, before]).wait()
            own = part[block, place].astype(F32)
            total = (slots[block, before].astype(F32) + own).astype(BF)

            @pl.when(hop < n - 1)
            def _():
                slots[block, before] = total
                copy(block, hop, slots.at[block, before]).start()

            @pl.when(hop == n - 1)
            def _():
                col = block % 4 * (model // 4) + block // 4 * width
                out_ref[:, col : col + width] = total

    @pl.when(step < blocks)
    def _():
        nibble = step % 4
        mask = 15 << (4 * nibble)
        unit = jnp.where(nibble < 2, jnp.where(nibble == 0, 1.0, 16.0), jnp.where(nibble == 2, 256.0, 4096.0))
        down = jnp.where(
            nibble < 2, jnp.where(nibble == 0, 1.0, 1 / 16), jnp.where(nibble == 2, 1 / 256, 1 / 4096)
        )
        first = nibble * (groups // 4) + step // 4 * (width // group)
        piece = min(512, units)
        for which, codes_ref, scale_ref in ((0, gc_ref, gs_ref), (1, uc_ref, us_ref)):
            for sub in range(width // group):
                for col in range(0, units, piece):
                    cols = slice(col, col + piece)
                    scale = scale_ref[pl.ds(first + sub, 1), cols] * down
                    scale = jnp.broadcast_to(scale, (16, piece))
                    for row in range(sub * group, (sub + 1) * group, 16):
                        at = slice(row, row + 16)
                        level = (codes_ref[at, cols] & mask).astype(F32) - 7.5 * unit
                        weights[which, at, cols] = (level * scale).astype(BF)
        total = lax.dot_general(gg_ref[...], weights[0], NT, preferred_element_type=F32)
        total += lax.dot_general(ug_ref[...], weights[1], NT, preferred_element_type=F32)
        total = total.astype(BF)
        for k, offset in enumerate(sequence):
            part[step, offset % n] = total[k * rows : (k + 1) * rows]


def input_scatter(gg, ug, gate_codes, up_codes, gate_scale, up_scale, sequence):
    tokens, units = gg.shape
    n = len(sequence)
    model = 4 * gate_codes.shape[0]
    rows = tokens // n
    blocks = 8
    width = model // blocks
    once = pl.Buffered(1)
    g_spec = pl.BlockSpec((tokens, units), lambda i: (0, 0), pipeline_mode=once)
    c_spec = pl.BlockSpec((width, units), lambda i: (jnp.minimum(i, blocks - 1) // 4, 0))
    s_spec = pl.BlockSpec(gate_scale.shape, lambda i: (0, 0), pipeline_mode=once)
    return pl.pallas_call(
        functools.partial(scatter_kernel, n, blocks, sequence),
        grid=(blocks + n,),
        in_specs=[g_spec, g_spec, c_spec, c_spec, s_spec, s_spec],
        out_specs=pl.BlockSpec((rows, model), lambda i: (0, 0)),
        out_shape=jax.ShapeDtypeStruct((rows, model), BF),
        scratch_shapes=[
            pltpu.VMEM((blocks, n, rows, width), BF),
            pltpu.VMEM((blocks, n - 1, rows, width), BF),
            pltpu.VMEM((2, width, units), BF),
            pltpu.SemaphoreType.DMA((blocks, n - 1)),
            pltpu.SemaphoreType.DMA((blocks, n - 1)),
        ],
        compiler_params=pltpu.CompilerParams(
            dimension_semantics=("arbitrary",),
            vmem_limit_bytes=60 * 1024 * 1024,
            collective_id=0,
            has_side_effects=True,
        ),
        cost_estimate=cost(4 * tokens * units * model, 2 * units * model),
        name="input_scatter",
    )(gg, ug, gate_codes, up_codes, gate_scale, up_scale)


def per_device(
    out_grad,
    gate_pre,
    up_pre,
    gate_codes,
    up_codes,
    down_codes,
    gate_scale,
    up_scale,
    down_scale,
    weak_weight,
    weak_index,
):
    n = lax.axis_size("tensor")
    groups = lax.axis_size("dp")
    half = n // 2
    rows, model = out_grad.shape
    middle = model // 2

    order = [2 * p if p < half else 2 * (n - 1 - p) + 1 for p in range(n)]
    to_right = [(order[p], order[(p + 1) % n]) for p in range(n)]
    to_left = [(order[(p + 1) % n], order[p]) for p in range(n)]
    me = lax.axis_index("tensor")
    position = ring_position(me, n)

    right = lambda x: lax.ppermute(x, "tensor", to_right)
    left = lambda x: lax.ppermute(x, "tensor", to_left)

    index = weak_index.astype(jnp.int32)
    weak32 = weak_weight.astype(F32)
    groups_down = down_scale.shape[0]
    cut = groups_down // 2
    down = functools.partial(deq_rows, down_codes, down_scale, weak32, index)

    blocks = {0: [(0, out_grad)]}
    from_left, from_right = out_grad, out_grad
    w_down = None
    for hop in range(1, half):
        from_left, from_right = right(from_left), left(from_right)
        if hop <= 2:
            w_down = down(0, cut) if hop == 1 else down(cut, groups_down - cut, w_down)
            from_left, from_right, w_down = lax.optimization_barrier(
                (from_left, from_right, w_down)
            )
        blocks[-hop] = [(0, from_left)]
        blocks[hop] = [(0, from_right)]

    sequence = [o for hop in range(1, half) for o in (-hop, hop)] + [half, 0]
    grads, weak = (), None
    for chunk in range(2):
        offsets = sequence[chunk * half : (chunk + 1) * half]
        if half in offsets:
            if grads:
                from_left, from_right, *grads = lax.optimization_barrier(
                    (from_left, from_right, *grads)
                )
            blocks[half] = [
                (0, right(from_left[:, :middle])),
                (middle, left(from_right[:, middle:])),
            ]
        places, pieces = [], []
        for k, offset in enumerate(offsets):
            for col, piece in blocks[offset]:
                places.append((k, col))
                pieces.append(piece)
        ids = jnp.stack([ring_device((position + o + n) % n, n) for o in offsets])
        gg, ug, sums = hidden_stage(
            chunk, 2, ids, places, pieces, w_down, index[:, None], gate_pre, up_pre, grads
        )
        grads = (gg, ug)
        weak = sums if weak is None else weak + sums
    in_grad = input_scatter(*grads, gate_codes, up_codes, gate_scale, up_scale, sequence)

    slots = weak.shape[0]
    mine = lax.axis_index("dp")
    width = model // groups
    columns = lambda g: lax.dynamic_slice(weak, (0, g * width), (slots, width))
    total = columns(mine)
    for shift in range(1, groups):
        sent = columns((mine + shift) % groups).astype(BF)
        total += lax.ppermute(
            sent, "dp", [(g, (g + shift) % groups) for g in range(groups)]
        ).astype(F32)
    factor = (gate_pre.shape[0] * groups) ** (-0.5)
    return in_grad, total * factor


def solution(mesh):
    in_specs = (
        P(("dp", "tensor"), None),
        P("dp", "tensor"),
        P("dp", "tensor"),
        P(None, "tensor"),
        P(None, "tensor"),
        P("tensor", None),
        P(None, "tensor"),
        P(None, "tensor"),
        P("tensor", None),
        P("tensor", None),
        P("tensor"),
    )
    out_specs = (P(("dp", "tensor"), None), P("tensor", "dp"))
    return jax.shard_map(
        per_device, mesh=mesh, in_specs=in_specs, out_specs=out_specs, check_vma=False
    )
```

```python
import functools

import jax
import jax.numpy as jnp
from jax import lax
from jax.experimental import pallas as pl
from jax.experimental.pallas import tpu as pltpu
from jax.sharding import PartitionSpec as P

BF = jnp.bfloat16
F32 = jnp.float32
NT = (((1,), (1,)), ((), ()))


def params(mib=60):
    return pltpu.CompilerParams(
        dimension_semantics=("arbitrary",), vmem_limit_bytes=mib * 1024 * 1024
    )


def cost(flops, nbytes, trans=0):
    return pl.CostEstimate(flops=flops, bytes_accessed=nbytes, transcendentals=trans)


def deq_rows_kernel(first, index_ref, codes_ref, scale_ref, weak_ref, *refs):
    out_ref = refs[-1]
    block = pl.program_id(0) + first
    rows, packed = codes_ref.shape
    slots, model = weak_ref.shape
    piece = min(512, packed)
    for nibble in range(4):
        unit = 16.0**nibble
        for col in range(0, packed, piece):
            cols = slice(col, col + piece)
            outs = slice(nibble * packed + col, nibble * packed + col + piece)
            scale = jnp.broadcast_to(scale_ref[pl.ds(block, 1), outs] * (1.0 / unit), (16, piece))
            for row in range(0, rows, 16):
                at = slice(row, row + 16)
                level = (codes_ref[at, cols] & (15 << (4 * nibble))).astype(F32) - 7.5 * unit
                out_ref[at, outs] = (level * scale).astype(BF)

    @pl.loop(0, slots)
    def _(slot):
        unit = index_ref[slot] - block * rows

        @pl.when((unit >= 0) & (unit < rows))
        def _():
            at = pl.ds(pl.multiple_of(unit // 16 * 16, 16), 16)
            hit = lax.broadcasted_iota(jnp.int32, (16, piece), 0) == unit % 16
            for col in range(0, model, piece):
                cols = slice(col, col + piece)
                row = jnp.broadcast_to(weak_ref[pl.ds(slot, 1), cols], (16, piece))
                out_ref[at, cols] = jnp.where(hit, row, out_ref[at, cols].astype(F32)).astype(BF)


def deq_rows(codes, scale, weak, index, first, count, before=None):
    units, packed = codes.shape
    groups, width = scale.shape
    group = units // groups
    slots = weak.shape[0]
    more = [] if before is None else [before]
    return pl.pallas_call(
        functools.partial(deq_rows_kernel, first),
        grid_spec=pltpu.PrefetchScalarGridSpec(
            num_scalar_prefetch=1,
            grid=(count,),
            in_specs=[
                pl.BlockSpec((group, packed), lambda r, index: (r + first, 0)),
                pl.BlockSpec((groups, width), lambda r, index: (0, 0)),
                pl.BlockSpec((slots, width), lambda r, index: (0, 0)),
            ]
            + [pl.BlockSpec(memory_space=pl.ANY)] * len(more),
            out_specs=pl.BlockSpec((group, width), lambda r, index: (r + first, 0)),
        ),
        out_shape=jax.ShapeDtypeStruct((units, width), BF),
        input_output_aliases={4: 0} if more else {},
        compiler_params=params(),
        cost_estimate=cost(count * group * width * 8, count * group * packed * 12),
        name="deq_rows",
    )(index, codes, scale, weak, *more)


def hidden_kernel(places, count, rows, *refs):
    pieces = refs[1 : 1 + len(places)]
    rest = refs[1 + len(places) :]
    w_ref, col_ref = rest[0], rest[1]
    gates = rest[2 : 2 + count]
    ups = rest[2 + count : 2 + 2 * count]
    gg_ref, ug_ref, weak_ref, tokens, picked = rest[-5:]
    step = pl.program_id(0)
    width = w_ref.shape[0]
    slots = col_ref.shape[0]

    @pl.when(step == 0)
    def _():
        for (row, col), piece in zip(places, pieces):
            tokens[row * rows : (row + 1) * rows, col : col + piece.shape[1]] = piece[...]
        picked[...] = jnp.zeros_like(picked)

    grad = lax.dot_general(tokens[...], w_ref[...], NT, preferred_element_type=F32)
    unit = lax.broadcasted_iota(jnp.int32, (slots, width), 1) + step * width
    onehot = (unit == col_ref[...]).astype(F32).astype(BF)
    hiddens = []
    for k in range(count):
        mine = slice(k * rows, (k + 1) * rows)
        gate = gates[k][...].astype(F32)
        up = ups[k][...].astype(F32)
        sig = 1.0 / (1.0 + jnp.exp(-gate))
        act = gate * sig
        part = grad[mine]
        ug_ref[mine, :] = (part * act).astype(BF)
        gg_ref[mine, :] = (part * up * sig * (1.0 + gate * (1.0 - sig))).astype(BF)
        hiddens.append((act * up).astype(BF))
    hidden = jnp.concatenate(hiddens, axis=0)
    picked[...] += lax.dot_general(onehot, hidden, NT, preferred_element_type=F32)

    @pl.when(step == pl.num_programs(0) - 1)
    def _():
        weak_ref[...] = jnp.dot(
            picked[...].astype(BF), tokens[...], preferred_element_type=F32
        )


def hidden_stage(chunk, chunks, ids, places, pieces, w_down, index_col, gate_pre, up_pre, before=()):
    count = ids.shape[0]
    rows = pieces[0].shape[0]
    units, model = w_down.shape
    slots = index_col.shape[0]
    width = min(256, units)
    total = count * rows
    pre_specs = [
        pl.BlockSpec((rows, width), functools.partial(lambda k, f, who: (who[k], f), k))
        for k in range(count)
    ]
    return pl.pallas_call(
        functools.partial(hidden_kernel, places, count, rows),
        grid_spec=pltpu.PrefetchScalarGridSpec(
            num_scalar_prefetch=1,
            grid=(units // width,),
            in_specs=[pl.BlockSpec(p.shape, lambda f, who: (0, 0)) for p in pieces]
            + [
                pl.BlockSpec((width, model), lambda f, who: (f, 0)),
                pl.BlockSpec((slots, 1), lambda f, who: (0, 0)),
            ]
            + pre_specs
            + pre_specs
            + [pl.BlockSpec(memory_space=pl.ANY)] * len(before),
            out_specs=[
                pl.BlockSpec((total, width), lambda f, who: (chunk, f)),
                pl.BlockSpec((total, width), lambda f, who: (chunk, f)),
                pl.BlockSpec((slots, model), lambda f, who: (0, 0)),
            ],
            scratch_shapes=[pltpu.VMEM((total, model), BF), pltpu.VMEM((slots, total), F32)],
        ),
        out_shape=[
            jax.ShapeDtypeStruct((chunks * total, units), BF),
            jax.ShapeDtypeStruct((chunks * total, units), BF),
            jax.ShapeDtypeStruct((slots, model), F32),
        ],
        input_output_aliases={3 + len(pieces) + 2 * count + k: k for k in range(len(before))},
        compiler_params=params(),
        cost_estimate=cost(
            2 * total * units * model, 2 * (units * model + 4 * total * units), total * units * 2
        ),
        name="hidden_stage",
    )(ids, *pieces, w_down, index_col, *([gate_pre] * count), *([up_pre] * count), *before)


def ring_device(p, n):
    back = p // (n // 2)
    return (1 - back) * (2 * p) + back * (2 * (n - 1 - p) + 1)


def ring_position(index, n):
    odd = index % 2
    return (1 - odd) * (index // 2) + odd * (n - 1 - index // 2)


def scatter_kernel(
    n,
    blocks,
    sequence,
    gg_ref,
    ug_ref,
    gc_ref,
    uc_ref,
    gs_ref,
    us_ref,
    out_ref,
    part,
    slots,
    weights,
    send_sem,
    recv_sem,
):
    step = pl.program_id(0)
    rows, model = out_ref.shape
    width, units = gc_ref.shape
    groups = gs_ref.shape[0]
    group = model // groups
    position = ring_position(lax.axis_index("tensor"), n)
    right = ring_device((position + 1) % n, n)
    left = ring_device((position + n - 1) % n, n)

    @pl.when(step == 0)
    def _():
        barrier = pltpu.get_barrier_semaphore()
        for other in (left, right):
            pl.semaphore_signal(
                barrier, inc=1, device_id={"tensor": other}, device_id_type=pl.DeviceIdType.MESH
            )
        pl.semaphore_wait(barrier, 2)

    def rightward(block):
        return block // 2 % 2 == 0

    def copy(block, hop, source):
        return pltpu.make_async_remote_copy(
            src_ref=source,
            dst_ref=slots.at[block, hop],
            send_sem=send_sem.at[block, hop],
            recv_sem=recv_sem.at[block, hop],
            device_id={"tensor": right if rightward(block) else left},
            device_id_type=pl.DeviceIdType.MESH,
        )

    for block in range(blocks):
        since = step - 1 - block
        hop = since // 2
        turn = (since >= 0) & (since % 2 == 0)
        place = (n - 1 - hop) if rightward(block) else (hop + 1) % n

        @pl.when(since == 0)
        def _():
            copy(block, 0, part.at[block, n - 1 if rightward(block) else 1]).start()

        @pl.when(turn & (hop > 0) & (hop < n))
        def _():
            before = hop - 1
            copy(block, before, slots.at[block, before]).wait()
            own = part[block, place].astype(F32)
            total = (slots[block, before].astype(F32) + own).astype(BF)

            @pl.when(hop < n - 1)
            def _():
                slots[block, before] = total
                copy(block, hop, slots.at[block, before]).start()

            @pl.when(hop == n - 1)
            def _():
                col = block % 4 * (model // 4) + block // 4 * width
                out_ref[:, col : col + width] = total

    @pl.when(step < blocks)
    def _():
        nibble = step % 4
        mask = 15 << (4 * nibble)
        unit = jnp.where(nibble < 2, jnp.where(nibble == 0, 1.0, 16.0), jnp.where(nibble == 2, 256.0, 4096.0))
        down = jnp.where(
            nibble < 2, jnp.where(nibble == 0, 1.0, 1 / 16), jnp.where(nibble == 2, 1 / 256, 1 / 4096)
        )
        first = nibble * (groups // 4) + step // 4 * (width // group)
        piece = min(512, units)
        for which, codes_ref, scale_ref in ((0, gc_ref, gs_ref), (1, uc_ref, us_ref)):
            for sub in range(width // group):
                for col in range(0, units, piece):
                    cols = slice(col, col + piece)
                    scale = scale_ref[pl.ds(first + sub, 1), cols] * down
                    scale = jnp.broadcast_to(scale, (16, piece))
                    for row in range(sub * group, (sub + 1) * group, 16):
                        at = slice(row, row + 16)
                        level = (codes_ref[at, cols] & mask).astype(F32) - 7.5 * unit
                        weights[which, at, cols] = (level * scale).astype(BF)
        total = lax.dot_general(gg_ref[...], weights[0], NT, preferred_element_type=F32)
        total += lax.dot_general(ug_ref[...], weights[1], NT, preferred_element_type=F32)
        total = total.astype(BF)
        for k, offset in enumerate(sequence):
            part[step, offset % n] = total[k * rows : (k + 1) * rows]


def input_scatter(gg, ug, gate_codes, up_codes, gate_scale, up_scale, sequence):
    tokens, units = gg.shape
    n = len(sequence)
    model = 4 * gate_codes.shape[0]
    rows = tokens // n
    blocks = 8
    width = model // blocks
    once = pl.Buffered(1)
    g_spec = pl.BlockSpec((tokens, units), lambda i: (0, 0), pipeline_mode=once)
    c_spec = pl.BlockSpec((width, units), lambda i: (jnp.minimum(i, blocks - 1) // 4, 0))
    s_spec = pl.BlockSpec(gate_scale.shape, lambda i: (0, 0), pipeline_mode=once)
    return pl.pallas_call(
        functools.partial(scatter_kernel, n, blocks, sequence),
        grid=(blocks + 2 * n - 1,),
        in_specs=[g_spec, g_spec, c_spec, c_spec, s_spec, s_spec],
        out_specs=pl.BlockSpec((rows, model), lambda i: (0, 0)),
        out_shape=jax.ShapeDtypeStruct((rows, model), BF),
        scratch_shapes=[
            pltpu.VMEM((blocks, n, rows, width), BF),
            pltpu.VMEM((blocks, n - 1, rows, width), BF),
            pltpu.VMEM((2, width, units), BF),
            pltpu.SemaphoreType.DMA((blocks, n - 1)),
            pltpu.SemaphoreType.DMA((blocks, n - 1)),
        ],
        compiler_params=pltpu.CompilerParams(
            dimension_semantics=("arbitrary",),
            vmem_limit_bytes=60 * 1024 * 1024,
            collective_id=0,
            has_side_effects=True,
        ),
        cost_estimate=cost(4 * tokens * units * model, 2 * units * model),
        name="input_scatter",
    )(gg, ug, gate_codes, up_codes, gate_scale, up_scale)


def per_device(
    out_grad,
    gate_pre,
    up_pre,
    gate_codes,
    up_codes,
    down_codes,
    gate_scale,
    up_scale,
    down_scale,
    weak_weight,
    weak_index,
):
    n = lax.axis_size("tensor")
    groups = lax.axis_size("dp")
    half = n // 2
    rows, model = out_grad.shape
    middle = model // 2

    order = [2 * p if p < half else 2 * (n - 1 - p) + 1 for p in range(n)]
    to_right = [(order[p], order[(p + 1) % n]) for p in range(n)]
    to_left = [(order[(p + 1) % n], order[p]) for p in range(n)]
    me = lax.axis_index("tensor")
    position = ring_position(me, n)

    right = lambda x: lax.ppermute(x, "tensor", to_right)
    left = lambda x: lax.ppermute(x, "tensor", to_left)

    index = weak_index.astype(jnp.int32)
    weak32 = weak_weight.astype(F32)
    groups_down = down_scale.shape[0]
    cut = groups_down // 2
    down = functools.partial(deq_rows, down_codes, down_scale, weak32, index)

    blocks = {0: [(0, out_grad)]}
    from_left, from_right = out_grad, out_grad
    w_down = None
    for hop in range(1, half):
        from_left, from_right = right(from_left), left(from_right)
        if hop <= 2:
            w_down = down(0, cut) if hop == 1 else down(cut, groups_down - cut, w_down)
            from_left, from_right, w_down = lax.optimization_barrier(
                (from_left, from_right, w_down)
            )
        blocks[-hop] = [(0, from_left)]
        blocks[hop] = [(0, from_right)]

    sequence = [o for hop in range(1, half) for o in (-hop, hop)] + [half, 0]
    grads, weak = (), None
    for chunk in range(2):
        offsets = sequence[chunk * half : (chunk + 1) * half]
        if half in offsets:
            if grads:
                from_left, from_right, *grads = lax.optimization_barrier(
                    (from_left, from_right, *grads)
                )
            blocks[half] = [
                (0, right(from_left[:, :middle])),
                (middle, left(from_right[:, middle:])),
            ]
        places, pieces = [], []
        for k, offset in enumerate(offsets):
            for col, piece in blocks[offset]:
                places.append((k, col))
                pieces.append(piece)
        ids = jnp.stack([ring_device((position + o + n) % n, n) for o in offsets])
        gg, ug, sums = hidden_stage(
            chunk, 2, ids, places, pieces, w_down, index[:, None], gate_pre, up_pre, grads
        )
        grads = (gg, ug)
        weak = sums if weak is None else weak + sums
    in_grad = input_scatter(*grads, gate_codes, up_codes, gate_scale, up_scale, sequence)

    slots = weak.shape[0]
    mine = lax.axis_index("dp")
    width = model // groups
    columns = lambda g: lax.dynamic_slice(weak, (0, g * width), (slots, width))
    total = columns(mine)
    for shift in range(1, groups):
        sent = columns((mine + shift) % groups).astype(BF)
        total += lax.ppermute(
            sent, "dp", [(g, (g + shift) % groups) for g in range(groups)]
        ).astype(F32)
    factor = (gate_pre.shape[0] * groups) ** (-0.5)
    return in_grad, total * factor


def solution(mesh):
    in_specs = (
        P(("dp", "tensor"), None),
        P("dp", "tensor"),
        P("dp", "tensor"),
        P(None, "tensor"),
        P(None, "tensor"),
        P("tensor", None),
        P(None, "tensor"),
        P(None, "tensor"),
        P("tensor", None),
        P("tensor", None),
        P("tensor"),
    )
    out_specs = (P(("dp", "tensor"), None), P("tensor", "dp"))
    return jax.shard_map(
        per_device, mesh=mesh, in_specs=in_specs, out_specs=out_specs, check_vma=False
    )
```
